32 devices in a mesh: users: 2 (over x), hist: 8 (over z, y), head: 2 (over core).
Axes of the slice: x: 2, y: 2, z: 4, core: 2. Of those that a mesh axis runs over, the one named last changes fastest.
Arguments:
- candidates: bfloat16 [2048, 512], P(('users', 'hist')), parts along dimension 0, may hold values from -6 to 6
- key_cache: bfloat16 [2, 32768, 512], P(None, ('users', 'hist'), 'head'), parts along dimension 1, may hold values from -6 to 6
- value_cache: bfloat16 [2, 32768, 512], P(None, ('users', 'hist'), 'head'), parts along dimension 1, may hold values from -6 to 6
- w_in: bfloat16 [2, 512, 4, 512], P(None, None, None, 'head'), may hold values from -0.25 to 0.25
- w_out: bfloat16 [2, 512, 512], P(None, 'head'), may hold values from -0.25 to 0.25
- rab_table: float32 [2, 32, 8], P(None, None, 'head'), may hold values from -4 to 4
- hist_len: int32 [16], P(('users', 'hist')), parts along dimension 0, may hold values from 1 to 2048, 8192 in all
- hist_bucket: int32 [32768], P(('users', 'hist')), parts along dimension 0, may hold values from 0 to 31
- visible: int32 [8, 128], P(None, ('users', 'hist')), parts along dimension 1, may hold values 0 or 1
Outputs:
- candidate_out: bfloat16 [2048, 512], P(('users', 'hist')), parts along dimension 0
The draws below stay inside these ranges and needn't reach their ends.
There are 2 independent parts, one for each index of `users`. The reference program is written for one: setup_inputs(seed, part) draws one part's arguments, and reference() takes and returns one part's arrays. A program takes and returns all parts, laid end to end along the dimension named above; an argument that names none is the same for every part. Nothing has to cross between parts.
Inputs may be any that keep to these rules, and one draw needn't show every extreme that they name: `hist_len`: entry s counts the valid events at the start of history shard s; the entries sum to 8192 and the largest is 2048. visible[m, b] is 1 where microbatch m sees history events b * 256 to (b + 1) * 256 - 1.
All inputs are finite; a program needn't handle non-finite values.
Results may differ from the reference program's by a relative error of at most 0.019.
Values may be sent and summed in bfloat16 or wider, within the bound.
A program may use at most 64 MiB of HBM per device.

```python
import math
import jax
import jax.numpy as jnp
import numpy as np
from jax import lax

D = 512
HEADS = 8
DH = 64
LAYERS = 2
NB = 32
BLOCK = 256
MICRO = 8
C = 1024
HIST_DEV = 2048
HIST = 16384
N_HIST = 8


def plant(array, rng, least, high):
    spot = [jax.random.randint(jax.random.fold_in(rng, axis), (), 0, length) for axis, length in enumerate(array.shape)]
    widest = array.shape.index(max(array.shape))
    next_to = spot[:widest] + [(spot[widest] + 1) % array.shape[widest]] + spot[widest + 1:]
    return array.at[tuple(spot)].set(least).at[tuple(next_to)].set(high)


def steps_of(rng, extent, split, low, top_value):
    loudness, own = 1.0, jax.random.fold_in(rng, 6)
    for position, parts in split:
        steps = jnp.exp(jax.random.uniform(jax.random.fold_in(own, position), (parts,), jnp.float32, low / len(split), top_value / len(split)))
        loudness = loudness * jnp.repeat(steps, extent[position] // parts).reshape([-1 if axis == position else 1 for axis in range(len(extent))])
    return loudness


def length_profile(amount, total, bound, lean):
    portions = [(1 << 20) // math.isqrt(grade ** lean) + 1 for grade in range(2, amount + 1)]
    spare, given = total - bound - (amount - 1), [1] * (amount - 1)
    while spare > 0:
        free = [i for i in range(amount - 1) if given[i] < bound]
        pool, budget = sum([portions[i] for i in free]), spare
        for i in free:
            extra = min(bound - given[i], max(1, budget * portions[i] // pool), spare)
            given[i] = given[i] + extra
            spare = spare - extra
    return np.array([bound] + given)


def uneven(own_key, amount, total, bound, lean):
    if amount == 2:
        one = jax.random.randint(own_key, (), max(1, total - bound), min(bound, total - 1) + 1)
        return jnp.stack([one, total - one])
    sizes = jnp.asarray(length_profile(amount, total, bound, lean), jnp.int32)
    twos = (amount - 1) // 2
    source_of, sink = sizes[1:1 + 2 * twos:2], sizes[2:2 + 2 * twos:2]
    slack = jnp.minimum(source_of - 1, bound - sink)
    shifted = jax.random.randint(jax.random.fold_in(own_key, 1), (twos,), 0, 1 << 20) % (slack + 1)
    sizes = sizes.at[1:1 + 2 * twos:2].set(source_of - shifted).at[2:2 + 2 * twos:2].set(sink + shifted)
    return sizes[jax.random.permutation(jax.random.fold_in(own_key, 2), amount)]


def bell_draw(rng, dims, deviation, reach, cuts=(), kind=jnp.bfloat16):
    result = deviation * jax.random.normal(rng, dims, jnp.float32)
    if cuts:
        result = result * steps_of(rng, dims, cuts, -0.22, 0.18)
    return jnp.clip(result, -reach, reach).astype(kind)


def setup_inputs(seed: int = 0, part: int = 0) -> dict:
    key_of = jax.random.split(jax.random.key(seed), 10)
    part_keys = jax.random.split(jax.random.fold_in(key_of[9], part), 10)
    candidates = bell_draw(part_keys[0], (C, D), 1.0, 6.0, ((0, 8),))
    key_cache = bell_draw(part_keys[1], (LAYERS, HIST, HEADS * DH), 1.0, 6.0, ((1, 8), (2, 2)))
    value_cache = bell_draw(part_keys[2], (LAYERS, HIST, HEADS * DH), 1.0, 6.0, ((1, 8), (2, 2)))
    w_in = bell_draw(key_of[3], (LAYERS, D, 4, HEADS * DH), D ** -0.5, 0.25, ((3, 2),))
    w_out = bell_draw(key_of[4], (LAYERS, HEADS * DH, D), (HEADS * DH) ** -0.5, 0.25, ((1, 2),))
    rab_table = bell_draw(key_of[5], (LAYERS, NB, HEADS), 1.0, 4.0, ((2, 2),), jnp.float32)
    hist_len = uneven(part_keys[6], N_HIST, N_HIST * HIST_DEV // 2, HIST_DEV, 2).astype(jnp.int32)
    hist_bucket = plant(jax.random.randint(part_keys[7], (HIST,), 0, NB), jax.random.fold_in(part_keys[7], 1), 0, NB - 1).astype(jnp.int32)
    visible = plant((jax.random.randint(part_keys[8], (MICRO, HIST // BLOCK), 0, 4) < 3).astype(jnp.int32), jax.random.fold_in(part_keys[8], 1), 0, 1)
    return dict(candidates=candidates, key_cache=key_cache, value_cache=value_cache, w_in=w_in, w_out=w_out, rab_table=rab_table, hist_len=hist_len, hist_bucket=hist_bucket, visible=visible)


epsilon = 1e-05

def reference(candidates, key_cache, value_cache, w_in, w_out, rab_table, hist_len, hist_bucket, visible):
    width = HEADS * DH
    factor = DH ** (-0.5)
    stream = candidates.astype(jnp.float32)
    micro_ids = jnp.arange(C, dtype=jnp.int32) // (C // MICRO)
    blocks_shard = HIST_DEV // BLOCK
    for layer_index in range(LAYERS):
        average = lax.optimization_barrier(jnp.mean(stream, axis=-1, keepdims=True))
        centred = stream - average
        variance = lax.optimization_barrier(jnp.mean(centred * centred, axis=-1, keepdims=True))
        normed = (centred * lax.rsqrt(variance + epsilon)).astype(jnp.bfloat16)
        projected = jnp.dot(normed, w_in[layer_index].reshape(D, 4 * width), preferred_element_type=jnp.float32)
        projected = jax.nn.silu(projected).astype(jnp.bfloat16).reshape(C, 4, width)
        queries = projected[:, 0].astype(jnp.float32).reshape(C, HEADS, DH)
        keys_new = projected[:, 1].astype(jnp.float32).reshape(C, HEADS, DH)
        values_new = projected[:, 2].astype(jnp.float32).reshape(C, HEADS, DH)
        gates = projected[:, 3].astype(jnp.float32)
        one_hot = (hist_bucket[:, None] == jnp.arange(NB, dtype=jnp.int32)[None, :]).astype(jnp.float32)
        bias = jnp.dot(one_hot, rab_table[layer_index], precision=lax.Precision.HIGHEST)
        cached_keys = key_cache[layer_index]
        cached_values = value_cache[layer_index]

        def shard_step(summed, shard):
            key_part = lax.dynamic_slice_in_dim(cached_keys, shard * HIST_DEV, HIST_DEV, 0).astype(jnp.float32).reshape(HIST_DEV, HEADS, DH)
            value_part = lax.dynamic_slice_in_dim(cached_values, shard * HIST_DEV, HIST_DEV, 0).astype(jnp.float32).reshape(HIST_DEV, HEADS, DH)
            bias_part = lax.dynamic_slice_in_dim(bias, shard * HIST_DEV, HIST_DEV, 0)
            visible_part = lax.dynamic_slice_in_dim(visible, shard * blocks_shard, blocks_shard, 1)[micro_ids]
            valid = (jnp.arange(HIST_DEV, dtype=jnp.int32) < hist_len[shard]).astype(jnp.float32)
            masking = jnp.repeat(visible_part, BLOCK, axis=1).astype(jnp.float32) * valid[None, :]
            scores = jnp.einsum('chd,khd->hck', queries, key_part) * factor + bias_part.T[:, None, :]
            weights = (jax.nn.silu(scores) * masking[None]).astype(jnp.bfloat16)
            weights = lax.optimization_barrier(weights).astype(jnp.float32)
            partial_value = jnp.einsum('hck,khd->chd', weights, value_part).astype(jnp.bfloat16)
            partial_value = lax.optimization_barrier(partial_value).astype(jnp.float32)
            return (summed + partial_value, None)
        history, _ = lax.scan(shard_step, jnp.zeros((C, HEADS, DH), jnp.float32), jnp.arange(N_HIST, dtype=jnp.int32))
        own_score = jax.nn.silu(lax.optimization_barrier(jnp.sum(queries * keys_new, axis=-1)) * factor)
        attended = (history + own_score[..., None] * values_new).reshape(C, width)
        average = lax.optimization_barrier(jnp.sum(attended, axis=-1, keepdims=True)) / width
        squares = lax.optimization_barrier(jnp.sum(attended * attended, axis=-1, keepdims=True)) / width
        normalized = (attended - average) * lax.rsqrt(squares - average * average + epsilon)
        gated = (normalized * gates).astype(jnp.bfloat16)
        stream = stream + jnp.dot(gated, w_out[layer_index], preferred_element_type=jnp.float32)
    return stream.astype(jnp.bfloat16)
```

```python
import functools

import jax
import jax.numpy as jnp
from jax import lax
from jax.experimental import pallas as pl
from jax.experimental.pallas import tpu as pltpu
from jax.sharding import PartitionSpec as P

DH = 64
BLOCK = 256
LANES = 128
PER = LANES // DH
GROUP_ROWS = 256
KEY_CHUNK = 512
BIG = 16384.0
MESH = pl.DeviceIdType.MESH

epsilon = 1e-05


def silu(v):
    return v / (1.0 + jnp.exp(-v))


def dot(a, b):
    return jnp.dot(a, b, preferred_element_type=jnp.float32)


def kernel(
    n,
    cand,
    w_in,
    key_hbm,
    val_hbm,
    w_out,
    rab,
    bucket,
    hlen,
    vis,
    out,
    keys,
    vals,
    kaug,
    table,
    events,
    w_other,
    qall,
    qaug,
    part,
    parts_in,
    acc,
    att_send,
    att_in,
    gate_send,
    gate_in,
    load_sem,
    q_send,
    q_recv,
    p_send,
    p_recv,
    h_send,
    h_recv,
):
    me = lax.axis_index("hist")
    other = 1 - lax.axis_index("head")
    layers, hist_dev, wl = key_hbm.shape
    rows, d = cand.shape
    heads = wl // DH
    pairs = wl // LANES
    nb = rab.shape[1]
    micro, blocks = vis.shape
    total = n * rows
    micro_rows = total // micro
    group_rows = min(GROUP_ROWS, total)
    per_group = group_rows // rows
    groups = n // per_group
    key_chunk = min(KEY_CHUNK, hist_dev)

    load_k = pltpu.make_async_copy(key_hbm, keys, load_sem.at[0])
    load_v = pltpu.make_async_copy(val_hbm, vals, load_sem.at[1])
    load_k.start()
    load_v.start()

    barrier = pltpu.get_barrier_semaphore()
    for j in range(1, n):
        pl.semaphore_signal(
            barrier, inc=1, device_id={"hist": lax.rem(me + j, n)}, device_id_type=MESH
        )
    pl.semaphore_signal(barrier, inc=1, device_id={"head": other}, device_id_type=MESH)

    def to_head(src, dst, index):
        return pltpu.make_async_remote_copy(
            src_ref=src,
            dst_ref=dst,
            send_sem=h_send.at[index],
            recv_sem=h_recv.at[index],
            device_id={"head": other},
            device_id_type=MESH,
        )

    def row_of(s):
        return pl.ds(pl.multiple_of(s * rows, rows), rows)

    def q_copy(l, s, owner):
        return pltpu.make_async_remote_copy(
            src_ref=qall.at[l, row_of(owner)],
            dst_ref=qall.at[l, row_of(owner)],
            send_sem=q_send.at[l, s],
            recv_sem=q_recv.at[l, owner],
            device_id={"hist": s},
            device_id_type=MESH,
        )

    def p_copy(l, s, owner):
        return pltpu.make_async_remote_copy(
            src_ref=part.at[l, row_of(s)],
            dst_ref=parts_in.at[l, owner],
            send_sem=p_send.at[l, s],
            recv_sem=p_recv.at[l, owner],
            device_id={"hist": s},
            device_id_type=MESH,
        )

    def build_keys():
        lane = lax.broadcasted_iota(jnp.int32, (LANES, LANES), 1)
        lane8 = lax.broadcasted_iota(jnp.int32, (blocks, LANES), 1)
        row8 = lax.broadcasted_iota(jnp.int32, (blocks, LANES), 0)
        base_of = (DH, 0)
        seen = []
        gone = []
        for base in base_of:
            held = jnp.zeros((blocks, LANES), jnp.float32)
            for m in range(micro):
                column = jnp.zeros((blocks, LANES), jnp.float32)
                for b in range(blocks):
                    value = (vis[m, b] - 1).astype(jnp.float32) * BIG
                    column = jnp.where(row8 == b, value, column)
                held = jnp.where(lane8 == base + 2 + m, column, held)
            seen.append(held)
            is_micro = (lane8 >= base + 2) & (lane8 < base + 2 + micro)
            gone.append(jnp.where(is_micro & (row8 == 0), -BIG, 0.0))
        for l in range(layers):
            for h in range(heads):
                base = base_of[h % PER]
                half = rab[l][:, h : h + 1] * 0.5
                high = half.astype(jnp.bfloat16).astype(jnp.float32)
                low = half - high
                lane_nb = lane[:nb]
                bias = jnp.where(lane_nb == base, high, jnp.where(lane_nb == base + 1, low, 0.0))
                fill = jnp.zeros((LANES - nb - 2 * blocks, LANES), jnp.float32)
                whole = jnp.concatenate([bias, seen[h % PER], gone[h % PER], fill], axis=0)
                start = (l * heads + h) * LANES
                table[:, start : start + LANES] = whole.astype(jnp.bfloat16)

        row = lax.broadcasted_iota(jnp.int32, (LANES, key_chunk), 0)
        spot = lax.broadcasted_iota(jnp.int32, (LANES, key_chunk), 1)
        lane_k = lax.broadcasted_iota(jnp.int32, (key_chunk, LANES), 1)
        length = hlen[0]
        for c in range(hist_dev // key_chunk):
            span = slice(c * key_chunk, (c + 1) * key_chunk)
            place = spot + c * key_chunk
            here = (
                (row == bucket[:, span])
                | (row == nb + place // BLOCK)
                | ((row == nb + blocks) & (place >= length))
            )
            events[span, :] = jnp.where(here, 1.0, 0.0).T.astype(jnp.bfloat16)
        load_k.wait()

        def chunk(c, carry):
            span = pl.ds(pl.multiple_of(c * key_chunk, key_chunk), key_chunk)
            spread = events[span, :]
            for l in range(layers):
                for h in range(heads):
                    start = (l * heads + h) * LANES
                    extra = dot(spread, table[:, start : start + LANES])
                    p = h // PER
                    tile = keys[l, span, p * LANES : (p + 1) * LANES].astype(jnp.float32)
                    mine = (lane_k < DH) if h % PER == 0 else (lane_k >= DH)
                    kaug[l, h, span, :] = jnp.where(mine, tile, extra).astype(jnp.bfloat16)
            return carry

        lax.fori_loop(0, hist_dev // key_chunk, chunk, 0)

    lane_q = lax.broadcasted_iota(jnp.int32, (group_rows, LANES), 1)
    row_q = lax.broadcasted_iota(jnp.int32, (group_rows, LANES), 0)
    lane_a = lax.broadcasted_iota(jnp.int32, (group_rows, LANES), 1)

    def attend(l, g):
        span = pl.ds(pl.multiple_of(g * group_rows, group_rows), group_rows)
        which = (row_q + g * group_rows) // micro_rows
        for h in range(heads):
            p = h // PER
            base = DH if h % PER == 0 else 0
            tile = qall[l, span, p * LANES : (p + 1) * LANES].astype(jnp.float32)
            ones = (lane_q == base) | (lane_q == base + 1) | (lane_q == base + 2 + which)
            mine = (lane_q < DH) if h % PER == 0 else (lane_q >= DH)
            qaug[h] = jnp.where(mine, tile, jnp.where(ones, 1.0, 0.0)).astype(jnp.bfloat16)
        acc[...] = jnp.zeros_like(acc)

        def chunk(c, carry):
            keys_at = pl.ds(pl.multiple_of(c * key_chunk, key_chunk), key_chunk)
            for p in range(pairs):
                value = vals[l, keys_at, p * LANES : (p + 1) * LANES]
                found = []
                for e in range(PER):
                    h = p * PER + e
                    y = lax.dot_general(
                        qaug[h],
                        kaug[l, h, keys_at, :],
                        (((1,), (1,)), ((), ())),
                        preferred_element_type=jnp.float32,
                    ).astype(jnp.bfloat16)
                    weight = y * (jnp.tanh(y) + 1.0)
                    found.append(dot(weight, value))
                acc[:, p * LANES : (p + 1) * LANES] += jnp.where(lane_a < DH, found[0], found[1])
            return carry

        lax.fori_loop(0, hist_dev // key_chunk, chunk, 0)
        part[l, span, :] = acc[...].astype(jnp.bfloat16)

    block_row = lax.broadcasted_iota(jnp.int32, (wl, wl), 0) // DH
    block_col = lax.broadcasted_iota(jnp.int32, (wl, wl), 1) // DH
    same_head = jnp.where(block_row == block_col, 1.0, 0.0).astype(jnp.bfloat16)

    stream = cand[...].astype(jnp.float32)
    for l in range(layers):
        average = jnp.mean(stream, axis=-1, keepdims=True)
        centred = stream - average
        variance = jnp.mean(centred * centred, axis=-1, keepdims=True)
        normed = (centred * lax.rsqrt(variance + epsilon)).astype(jnp.bfloat16)

        def project(i):
            return silu(dot(normed, w_in[l, :, i * wl : (i + 1) * wl])).astype(jnp.bfloat16)

        queries = project(0).astype(jnp.float32)
        qall[l, row_of(me), :] = (queries * (0.5 * DH**-0.5)).astype(jnp.bfloat16)
        if l == 0:
            pl.semaphore_wait(barrier, n)
        for j in range(1, n):
            q_copy(l, lax.rem(me + j, n), me).start()
        keys_new = project(1).astype(jnp.float32)
        values_new = project(2).astype(jnp.float32)
        gates = project(3)
        gate_send[l] = gates
        gate_copy = to_head(gate_send.at[l], gate_in.at[l], 2 * l)
        gate_copy.start()
        if l == 0:
            w_copy = to_head(w_out, w_other, 2 * layers)
            w_copy.start()
        product = queries * keys_new
        high = product.astype(jnp.bfloat16)
        low = (product - high.astype(jnp.float32)).astype(jnp.bfloat16)
        own_score = dot(high, same_head) + dot(low, same_head)
        own = silu(own_score * (DH**-0.5)) * values_new
        if l == 0:
            build_keys()
            load_v.wait()

        def group(t, carry):
            g = lax.rem(me // per_group + t, groups)
            for i in range(per_group):
                s = g * per_group + i

                @pl.when(s != me)
                def _():
                    q_copy(l, s, s).wait_recv()

            attend(l, g)
            for i in range(per_group):
                s = g * per_group + i

                @pl.when(s != me)
                def _():
                    p_copy(l, s, me).start()

            return carry

        lax.fori_loop(0, groups, group, 0)
        history = part[l, row_of(me), :].astype(jnp.float32)
        for j in range(1, n):
            s = lax.rem(me + j, n)
            p_copy(l, s, s).wait_recv()
            history = history + parts_in[l, s].astype(jnp.float32)
        attended = history + own
        att_send[l] = attended
        att_copy = to_head(att_send.at[l], att_in.at[l], 2 * l + 1)
        att_copy.start()
        if l == 0:
            w_copy.wait_recv()
        gate_copy.wait_recv()
        att_copy.wait_recv()
        theirs = att_in[l]
        width = 2 * wl
        mean = (
            jnp.sum(attended, axis=-1, keepdims=True) + jnp.sum(theirs, axis=-1, keepdims=True)
        ) / width
        square = (
            jnp.sum(attended * attended, axis=-1, keepdims=True)
            + jnp.sum(theirs * theirs, axis=-1, keepdims=True)
        ) / width
        rstd = lax.rsqrt(square - mean * mean + epsilon)
        gated = ((attended - mean) * rstd * gates.astype(jnp.float32)).astype(jnp.bfloat16)
        gated_other = ((theirs - mean) * rstd * gate_in[l].astype(jnp.float32)).astype(
            jnp.bfloat16
        )
        stream = stream + (dot(gated, w_out[l]) + dot(gated_other, w_other[l]))
        gate_copy.wait_send()
        att_copy.wait_send()
        if l == 0:
            w_copy.wait_send()
        for j in range(1, n):
            s = lax.rem(me + j, n)
            q_copy(l, s, me).wait_send()
            p_copy(l, s, me).wait_send()
    out[...] = stream.astype(out.dtype)


def shards(
    n, candidates, key_cache, value_cache, w_in, w_out, rab_table, hist_len, hist_bucket, visible
):
    layers, hist_dev, wl = key_cache.shape
    rows, d = candidates.shape
    heads = wl // DH
    total = n * rows
    group_rows = min(GROUP_ROWS, total)
    bf16, f32 = jnp.bfloat16, jnp.float32
    vmem = pl.BlockSpec(memory_space=pltpu.VMEM)
    smem = pl.BlockSpec(memory_space=pltpu.SMEM)
    hbm = pl.BlockSpec(memory_space=pl.ANY)
    dma = pltpu.SemaphoreType.DMA
    return pl.pallas_call(
        functools.partial(kernel, n),
        out_shape=jax.ShapeDtypeStruct((rows, d), bf16),
        in_specs=[vmem, vmem, hbm, hbm, vmem, vmem, vmem, smem, smem],
        out_specs=vmem,
        scratch_shapes=[
            pltpu.VMEM((layers, hist_dev, wl), bf16),
            pltpu.VMEM((layers, hist_dev, wl), bf16),
            pltpu.VMEM((layers, heads, hist_dev, LANES), bf16),
            pltpu.VMEM((LANES, layers * heads * LANES), bf16),
            pltpu.VMEM((hist_dev, LANES), bf16),
            pltpu.VMEM(w_out.shape, bf16),
            pltpu.VMEM((layers, total, wl), bf16),
            pltpu.VMEM((heads, group_rows, LANES), bf16),
            pltpu.VMEM((layers, total, wl), bf16),
            pltpu.VMEM((layers, n, rows, wl), bf16),
            pltpu.VMEM((group_rows, wl), f32),
            pltpu.VMEM((layers, rows, wl), f32),
            pltpu.VMEM((layers, rows, wl), f32),
            pltpu.VMEM((layers, rows, wl), bf16),
            pltpu.VMEM((layers, rows, wl), bf16),
            dma((2,)),
            dma((layers, n)),
            dma((layers, n)),
            dma((layers, n)),
            dma((layers, n)),
            dma((2 * layers + 1,)),
            dma((2 * layers + 1,)),
        ],
        compiler_params=pltpu.CompilerParams(
            collective_id=0, has_side_effects=True, vmem_limit_bytes=48 * 1024 * 1024
        ),
    )(
        candidates,
        w_in.reshape(layers, d, 4 * wl),
        key_cache,
        value_cache,
        w_out,
        rab_table,
        hist_bucket.reshape(1, hist_dev),
        hist_len,
        visible,
    )


def solution(mesh):
    placed = (
        P(("users", "hist"), None),
        P(None, ("users", "hist"), "head"),
        P(None, ("users", "hist"), "head"),
        P(None, None, None, "head"),
        P(None, "head", None),
        P(None, None, "head"),
        P(("users", "hist")),
        P(("users", "hist")),
        P(None, ("users", "hist")),
    )
    return jax.shard_map(
        functools.partial(shards, mesh.shape["hist"]),
        mesh=mesh,
        in_specs=placed,
        out_specs=P(("users", "hist"), None),
        check_vma=False,
    )
```

```python
import functools

import jax
import jax.numpy as jnp
from jax import lax
from jax.experimental import pallas as pl
from jax.experimental.pallas import tpu as pltpu
from jax.sharding import PartitionSpec as P

DH = 64
BLOCK = 256
LANES = 128
PER = LANES // DH
GROUP_ROWS = 256
KEY_CHUNK = 1024
BIG = 16384.0
MESH = pl.DeviceIdType.MESH

epsilon = 1e-05


def silu(v):
    return v / (1.0 + jnp.exp(-v))


def dot(a, b):
    return jnp.dot(a, b, preferred_element_type=jnp.float32)


def kernel(
    n,
    inner,
    cand,
    w_in,
    key_hbm,
    val_hbm,
    w_out,
    rab,
    bucket,
    hlen,
    vis,
    out,
    keys,
    vals,
    kaug,
    table,
    events,
    w_other,
    qall,
    qaug,
    part,
    parts_in,
    pair_in,
    merged,
    acc,
    att_send,
    att_in,
    gate_send,
    gate_in,
    load_sem,
    q_send,
    q_recv,
    p_send,
    p_recv,
    f_send,
    y_send,
    y_recv,
    h_send,
    h_recv,
):
    me = lax.axis_index("hist")
    other = 1 - lax.axis_index("head")
    layers, hist_dev, wl = key_hbm.shape
    rows, d = cand.shape
    heads = wl // DH
    pairs = wl // LANES
    nb = rab.shape[1]
    micro, blocks = vis.shape
    total = n * rows
    micro_rows = total // micro
    group_rows = min(GROUP_ROWS, total)
    per_group = group_rows // rows
    groups = n // per_group
    outer = n // inner
    relay = inner == 2 and per_group == inner
    line, side = me // inner, lax.rem(me, inner)
    beside = line * inner + (inner - 1 - side)
    key_chunk = min(KEY_CHUNK, hist_dev)

    load_k = pltpu.make_async_copy(key_hbm, keys, load_sem.at[0])
    load_v = pltpu.make_async_copy(val_hbm, vals, load_sem.at[1])
    load_k.start()
    load_v.start()

    barrier = pltpu.get_barrier_semaphore()
    for j in range(1, n):
        pl.semaphore_signal(
            barrier, inc=1, device_id={"hist": lax.rem(me + j, n)}, device_id_type=MESH
        )
    pl.semaphore_signal(barrier, inc=1, device_id={"head": other}, device_id_type=MESH)

    def to_head(src, dst, index):
        return pltpu.make_async_remote_copy(
            src_ref=src,
            dst_ref=dst,
            send_sem=h_send.at[index],
            recv_sem=h_recv.at[index],
            device_id={"head": other},
            device_id_type=MESH,
        )

    def row_of(s):
        return pl.ds(pl.multiple_of(s * rows, rows), rows)

    def q_copy(l, s, owner):
        return pltpu.make_async_remote_copy(
            src_ref=qall.at[l, row_of(owner)],
            dst_ref=qall.at[l, row_of(owner)],
            send_sem=q_send.at[l, s],
            recv_sem=q_recv.at[l, owner],
            device_id={"hist": s},
            device_id_type=MESH,
        )

    def p_copy(l, s, owner):
        return pltpu.make_async_remote_copy(
            src_ref=part.at[l, row_of(s)],
            dst_ref=parts_in.at[l, owner],
            send_sem=p_send.at[l, s],
            recv_sem=p_recv.at[l, owner],
            device_id={"hist": s},
            device_id_type=MESH,
        )

    def f_copy(l, z, owner):
        return pltpu.make_async_remote_copy(
            src_ref=qall.at[l, row_of(owner)],
            dst_ref=qall.at[l, row_of(owner)],
            send_sem=f_send.at[l, z],
            recv_sem=q_recv.at[l, owner],
            device_id={"hist": beside},
            device_id_type=MESH,
        )

    def y_copy(l, z):
        return pltpu.make_async_remote_copy(
            src_ref=part.at[l, row_of(z * inner + (inner - 1 - side))],
            dst_ref=pair_in.at[l, z],
            send_sem=y_send.at[l, z],
            recv_sem=y_recv.at[l, z],
            device_id={"hist": beside},
            device_id_type=MESH,
        )

    def m_copy(l, z, owner):
        return pltpu.make_async_remote_copy(
            src_ref=merged.at[l, z],
            dst_ref=parts_in.at[l, owner],
            send_sem=p_send.at[l, z],
            recv_sem=p_recv.at[l, owner],
            device_id={"hist": z * inner + side},
            device_id_type=MESH,
        )

    def merge(l, z):
        y_copy(l, z).wait_recv()
        both = part[l, row_of(z * inner + side), :].astype(jnp.float32)
        both = both + pair_in[l, z].astype(jnp.float32)
        merged[l, z] = both.astype(jnp.bfloat16)
        m_copy(l, z, line).start()

    def build_keys():
        lane = lax.broadcasted_iota(jnp.int32, (LANES, LANES), 1)
        lane8 = lax.broadcasted_iota(jnp.int32, (blocks, LANES), 1)
        row8 = lax.broadcasted_iota(jnp.int32, (blocks, LANES), 0)
        base_of = (DH, 0)
        seen = []
        gone = []
        for base in base_of:
            held = jnp.zeros((blocks, LANES), jnp.float32)
            for m in range(micro):
                column = jnp.zeros((blocks, LANES), jnp.float32)
                for b in range(blocks):
                    value = (vis[m, b] - 1).astype(jnp.float32) * BIG
                    column = jnp.where(row8 == b, value, column)
                held = jnp.where(lane8 == base + 2 + m, column, held)
            seen.append(held)
            is_micro = (lane8 >= base + 2) & (lane8 < base + 2 + micro)
            gone.append(jnp.where(is_micro & (row8 == 0), -BIG, 0.0))
        for l in range(layers):
            for h in range(heads):
                base = base_of[h % PER]
                half = rab[l][:, h : h + 1] * 0.5
                high = half.astype(jnp.bfloat16).astype(jnp.float32)
                low = half - high
                lane_nb = lane[:nb]
                bias = jnp.where(lane_nb == base, high, jnp.where(lane_nb == base + 1, low, 0.0))
                fill = jnp.zeros((LANES - nb - 2 * blocks, LANES), jnp.float32)
                whole = jnp.concatenate([bias, seen[h % PER], gone[h % PER], fill], axis=0)
                start = (l * heads + h) * LANES
                table[:, start : start + LANES] = whole.astype(jnp.bfloat16)

        row = lax.broadcasted_iota(jnp.int32, (LANES, key_chunk), 0)
        spot = lax.broadcasted_iota(jnp.int32, (LANES, key_chunk), 1)
        lane_k = lax.broadcasted_iota(jnp.int32, (key_chunk, LANES), 1)
        length = hlen[0]
        for c in range(hist_dev // key_chunk):
            span = slice(c * key_chunk, (c + 1) * key_chunk)
            place = spot + c * key_chunk
            here = (
                (row == bucket[:, span])
                | (row == nb + place // BLOCK)
                | ((row == nb + blocks) & (place >= length))
            )
            events[span, :] = jnp.where(here, 1.0, 0.0).T.astype(jnp.bfloat16)
        load_k.wait()

        def chunk(c, carry):
            span = pl.ds(pl.multiple_of(c * key_chunk, key_chunk), key_chunk)
            spread = events[span, :]
            for l in range(layers):
                for h in range(heads):
                    start = (l * heads + h) * LANES
                    extra = dot(spread, table[:, start : start + LANES])
                    p = h // PER
                    tile = keys[l, span, p * LANES : (p + 1) * LANES].astype(jnp.float32)
                    mine = (lane_k < DH) if h % PER == 0 else (lane_k >= DH)
                    kaug[l, h, span, :] = jnp.where(mine, tile, extra).astype(jnp.bfloat16)
            return carry

        lax.fori_loop(0, hist_dev // key_chunk, chunk, 0)

    lane_q = lax.broadcasted_iota(jnp.int32, (group_rows, LANES), 1)
    row_q = lax.broadcasted_iota(jnp.int32, (group_rows, LANES), 0)
    lane_a = lax.broadcasted_iota(jnp.int32, (group_rows, LANES), 1)

    def attend(l, g, between):
        span = pl.ds(pl.multiple_of(g * group_rows, group_rows), group_rows)
        which = (row_q + g * group_rows) // micro_rows
        for h in range(heads):
            p = h // PER
            base = DH if h % PER == 0 else 0
            tile = qall[l, span, p * LANES : (p + 1) * LANES].astype(jnp.float32)
            ones = (lane_q == base) | (lane_q == base + 1) | (lane_q == base + 2 + which)
            mine = (lane_q < DH) if h % PER == 0 else (lane_q >= DH)
            qaug[h] = jnp.where(mine, tile, jnp.where(ones, 1.0, 0.0)).astype(jnp.bfloat16)
        acc[...] = jnp.zeros_like(acc)

        def chunk(c, carry):
            keys_at = pl.ds(pl.multiple_of(c * key_chunk, key_chunk), key_chunk)
            for p in range(pairs):
                value = vals[l, keys_at, p * LANES : (p + 1) * LANES]
                found = []
                for e in range(PER):
                    h = p * PER + e
                    y = lax.dot_general(
                        qaug[h],
                        kaug[l, h, keys_at, :],
                        (((1,), (1,)), ((), ())),
                        preferred_element_type=jnp.float32,
                    ).astype(jnp.bfloat16)
                    weight = y * (jnp.tanh(y) + 1.0)
                    found.append(dot(weight, value))
                acc[:, p * LANES : (p + 1) * LANES] += jnp.where(lane_a < DH, found[0], found[1])
            return carry

        steps = hist_dev // key_chunk
        lax.fori_loop(0, steps // 2, chunk, 0)
        between()
        lax.fori_loop(steps // 2, steps, chunk, 0)
        part[l, span, :] = acc[...].astype(jnp.bfloat16)

    block_row = lax.broadcasted_iota(jnp.int32, (wl, wl), 0) // DH
    block_col = lax.broadcasted_iota(jnp.int32, (wl, wl), 1) // DH
    same_head = jnp.where(block_row == block_col, 1.0, 0.0).astype(jnp.bfloat16)

    stream = cand[...].astype(jnp.float32)
    for l in range(layers):
        average = jnp.mean(stream, axis=-1, keepdims=True)
        centred = stream - average
        variance = jnp.mean(centred * centred, axis=-1, keepdims=True)
        normed = (centred * lax.rsqrt(variance + epsilon)).astype(jnp.bfloat16)

        def project(i):
            return silu(dot(normed, w_in[l, :, i * wl : (i + 1) * wl])).astype(jnp.bfloat16)

        queries = project(0).astype(jnp.float32)
        qall[l, row_of(me), :] = (queries * (0.5 * DH**-0.5)).astype(jnp.bfloat16)
        if l == 0:
            pl.semaphore_wait(barrier, n)
        if relay:
            q_copy(l, beside, me).start()
            for j in range(1, outer):
                q_copy(l, lax.rem(line + outer - j, outer) * inner + side, me).start()
        else:
            for j in range(1, n):
                q_copy(l, lax.rem(me + j, n), me).start()
        keys_new = project(1).astype(jnp.float32)
        values_new = project(2).astype(jnp.float32)
        gates = project(3)
        gate_send[l] = gates
        gate_copy = to_head(gate_send.at[l], gate_in.at[l], 2 * l)
        gate_copy.start()
        if l == 0:
            w_copy = to_head(w_out, w_other, 2 * layers)
            w_copy.start()
        product = queries * keys_new
        high = product.astype(jnp.bfloat16)
        low = (product - high.astype(jnp.float32)).astype(jnp.bfloat16)
        own_score = dot(high, same_head) + dot(low, same_head)
        own = silu(own_score * (DH**-0.5)) * values_new
        if l == 0:
            build_keys()
            load_v.wait()

        def group(t, carry):
            g = lax.rem(me // per_group + t, groups)
            for i in range(per_group):
                s = g * per_group + i

                @pl.when(s != me)
                def _():
                    q_copy(l, s, s).wait_recv()

            attend(l, g, lambda: None)
            for i in range(per_group):
                s = g * per_group + i

                @pl.when(s != me)
                def _():
                    p_copy(l, s, me).start()

            return carry

        def relayed(t, carry):
            z = lax.rem(line + t, outer)
            after = lax.rem(line + t + 1, outer)
            before = lax.rem(line + t + outer - 1, outer)
            q_copy(l, z * inner + (inner - 1 - side), z * inner + (inner - 1 - side)).wait_recv()

            def between():
                @pl.when(t < outer - 1)
                def _():
                    q_copy(l, after * inner + side, after * inner + side).wait_recv()
                    f_copy(l, after, after * inner + side).start()

                @pl.when(t > 1)
                def _():
                    merge(l, before)

            attend(l, z, between)
            y_copy(l, z).start()
            return carry

        if relay:
            lax.fori_loop(0, outer, relayed, 0)
            if outer > 1:
                merge(l, lax.rem(line + outer - 1, outer))
            y_copy(l, line).wait_recv()
            history = part[l, row_of(me), :].astype(jnp.float32)
            history = history + pair_in[l, line].astype(jnp.float32)
            for j in range(1, outer):
                z = lax.rem(line + outer - j, outer)
                m_copy(l, z, z).wait_recv()
                history = history + parts_in[l, z].astype(jnp.float32)
        else:
            lax.fori_loop(0, groups, group, 0)
            history = part[l, row_of(me), :].astype(jnp.float32)
            for j in range(1, n):
                s = lax.rem(me + j, n)
                p_copy(l, s, s).wait_recv()
                history = history + parts_in[l, s].astype(jnp.float32)
        attended = history + own
        att_send[l] = attended
        att_copy = to_head(att_send.at[l], att_in.at[l], 2 * l + 1)
        att_copy.start()
        if l == 0:
            w_copy.wait_recv()
        gate_copy.wait_recv()
        att_copy.wait_recv()
        theirs = att_in[l]
        width = 2 * wl
        mean = (
            jnp.sum(attended, axis=-1, keepdims=True) + jnp.sum(theirs, axis=-1, keepdims=True)
        ) / width
        square = (
            jnp.sum(attended * attended, axis=-1, keepdims=True)
            + jnp.sum(theirs * theirs, axis=-1, keepdims=True)
        ) / width
        rstd = lax.rsqrt(square - mean * mean + epsilon)
        gated = ((attended - mean) * rstd * gates.astype(jnp.float32)).astype(jnp.bfloat16)
        gated_other = ((theirs - mean) * rstd * gate_in[l].astype(jnp.float32)).astype(
            jnp.bfloat16
        )
        stream = stream + (dot(gated, w_out[l]) + dot(gated_other, w_other[l]))
        gate_copy.wait_send()
        att_copy.wait_send()
        if l == 0:
            w_copy.wait_send()
        if relay:
            q_copy(l, beside, me).wait_send()
            y_copy(l, line).wait_send()
            for j in range(1, outer):
                z = lax.rem(line + j, outer)
                q_copy(l, z * inner + side, me).wait_send()
                f_copy(l, z, z * inner + side).wait_send()
                y_copy(l, z).wait_send()
                m_copy(l, z, line).wait_send()
        else:
            for j in range(1, n):
                s = lax.rem(me + j, n)
                q_copy(l, s, me).wait_send()
                p_copy(l, s, me).wait_send()
    out[...] = stream.astype(out.dtype)


def shards(
    n, inner, candidates, key_cache, value_cache, w_in, w_out, rab_table, hist_len, hist_bucket, visible
):
    layers, hist_dev, wl = key_cache.shape
    rows, d = candidates.shape
    heads = wl // DH
    total = n * rows
    group_rows = min(GROUP_ROWS, total)
    bf16, f32 = jnp.bfloat16, jnp.float32
    vmem = pl.BlockSpec(memory_space=pltpu.VMEM)
    smem = pl.BlockSpec(memory_space=pltpu.SMEM)
    hbm = pl.BlockSpec(memory_space=pl.ANY)
    dma = pltpu.SemaphoreType.DMA
    return pl.pallas_call(
        functools.partial(kernel, n, inner),
        out_shape=jax.ShapeDtypeStruct((rows, d), bf16),
        in_specs=[vmem, vmem, hbm, hbm, vmem, vmem, vmem, smem, smem],
        out_specs=vmem,
        scratch_shapes=[
            pltpu.VMEM((layers, hist_dev, wl), bf16),
            pltpu.VMEM((layers, hist_dev, wl), bf16),
            pltpu.VMEM((layers, heads, hist_dev, LANES), bf16),
            pltpu.VMEM((LANES, layers * heads * LANES), bf16),
            pltpu.VMEM((hist_dev, LANES), bf16),
            pltpu.VMEM(w_out.shape, bf16),
            pltpu.VMEM((layers, total, wl), bf16),
            pltpu.VMEM((heads, group_rows, LANES), bf16),
            pltpu.VMEM((layers, total, wl), bf16),
            pltpu.VMEM((layers, n, rows, wl), bf16),
            pltpu.VMEM((layers, n // inner, rows, wl), bf16),
            pltpu.VMEM((layers, n // inner, rows, wl), bf16),
            pltpu.VMEM((group_rows, wl), f32),
            pltpu.VMEM((layers, rows, wl), f32),
            pltpu.VMEM((layers, rows, wl), f32),
            pltpu.VMEM((layers, rows, wl), bf16),
            pltpu.VMEM((layers, rows, wl), bf16),
            dma((2,)),
            dma((layers, n)),
            dma((layers, n)),
            dma((layers, n)),
            dma((layers, n)),
            dma((layers, n)),
            dma((layers, n)),
            dma((layers, n)),
            dma((2 * layers + 1,)),
            dma((2 * layers + 1,)),
        ],
        compiler_params=pltpu.CompilerParams(
            collective_id=0, has_side_effects=True, vmem_limit_bytes=48 * 1024 * 1024
        ),
    )(
        candidates,
        w_in.reshape(layers, d, 4 * wl),
        key_cache,
        value_cache,
        w_out,
        rab_table,
        hist_bucket.reshape(1, hist_dev),
        hist_len,
        visible,
    )


def inner_of(mesh):
    n = mesh.shape["hist"]
    if n % 2 or n < 4:
        return 1
    index = [slice(None) if name == "hist" else 0 for name in mesh.axis_names]
    spots = [getattr(device, "coords", None) for device in mesh.devices[tuple(index)][:3]]
    if any(spot is None for spot in spots):
        return 1
    apart = [sum(abs(a - b) for a, b in zip(spots[0], spot)) for spot in spots[1:]]
    return 2 if apart == [1, 1] else 1


def solution(mesh):
    placed = (
        P(("users", "hist"), None),
        P(None, ("users", "hist"), "head"),
        P(None, ("users", "hist"), "head"),
        P(None, None, None, "head"),
        P(None, "head", None),
        P(None, None, "head"),
        P(("users", "hist")),
        P(("users", "hist")),
        P(None, ("users", "hist")),
    )
    return jax.shard_map(
        functools.partial(shards, mesh.shape["hist"], inner_of(mesh)),
        mesh=mesh,
        in_specs=placed,
        out_specs=P(("users", "hist"), None),
        check_vma=False,
    )
```

```python
import functools

import jax
import jax.numpy as jnp
from jax import lax
from jax.experimental import pallas as pl
from jax.experimental.pallas import tpu as pltpu
from jax.sharding import PartitionSpec as P

DH = 64
BLOCK = 256
LANES = 128
PER = LANES // DH
GROUP_ROWS = 256
KEY_CHUNK = 2048
BIG = 16384.0
MESH = pl.DeviceIdType.MESH

epsilon = 1e-05


def silu(v):
    return v / (1.0 + jnp.exp(-v))


def dot(a, b):
    return jnp.dot(a, b, preferred_element_type=jnp.float32)


def kernel(
    n,
    inner,
    cand,
    w_in,
    key_hbm,
    val_hbm,
    w_out,
    rab,
    bucket,
    hlen,
    vis,
    out,
    keys,
    vals,
    kaug,
    table,
    events,
    w_other,
    qall,
    qaug,
    part,
    parts_in,
    pair_in,
    merged,
    acc,
    att_send,
    att_in,
    gate_send,
    gate_in,
    load_sem,
    q_send,
    q_recv,
    p_send,
    p_recv,
    y_send,
    y_recv,
    h_send,
    h_recv,
):
    me = lax.axis_index("hist")
    other = 1 - lax.axis_index("head")
    layers, hist_dev, wl = key_hbm.shape
    rows, d = cand.shape
    heads = wl // DH
    pairs = wl // LANES
    nb = rab.shape[1]
    micro, blocks = vis.shape
    total = n * rows
    micro_rows = total // micro
    group_rows = min(GROUP_ROWS, total)
    per_group = group_rows // rows
    groups = n // per_group
    outer = n // inner
    relay = inner == 2 and per_group == inner
    line, side = me // inner, lax.rem(me, inner)
    beside = line * inner + (inner - 1 - side)
    key_chunk = min(KEY_CHUNK, hist_dev)

    load_k = pltpu.make_async_copy(key_hbm, keys, load_sem.at[0])
    load_v = pltpu.make_async_copy(val_hbm, vals, load_sem.at[1])
    load_k.start()
    load_v.start()

    barrier = pltpu.get_barrier_semaphore()
    for j in range(1, n):
        pl.semaphore_signal(
            barrier, inc=1, device_id={"hist": lax.rem(me + j, n)}, device_id_type=MESH
        )
    pl.semaphore_signal(barrier, inc=1, device_id={"head": other}, device_id_type=MESH)

    def to_head(src, dst, index):
        return pltpu.make_async_remote_copy(
            src_ref=src,
            dst_ref=dst,
            send_sem=h_send.at[index],
            recv_sem=h_recv.at[index],
            device_id={"head": other},
            device_id_type=MESH,
        )

    def row_of(s):
        return pl.ds(pl.multiple_of(s * rows, rows), rows)

    def q_copy(l, s, owner):
        return pltpu.make_async_remote_copy(
            src_ref=qall.at[l, row_of(owner)],
            dst_ref=qall.at[l, row_of(owner)],
            send_sem=q_send.at[l, s],
            recv_sem=q_recv.at[l, owner],
            device_id={"hist": s},
            device_id_type=MESH,
        )

    def p_copy(l, s, owner):
        return pltpu.make_async_remote_copy(
            src_ref=part.at[l, row_of(s)],
            dst_ref=parts_in.at[l, owner],
            send_sem=p_send.at[l, s],
            recv_sem=p_recv.at[l, owner],
            device_id={"hist": s},
            device_id_type=MESH,
        )

    def y_copy(l, z):
        return pltpu.make_async_remote_copy(
            src_ref=part.at[l, row_of(z * inner + (inner - 1 - side))],
            dst_ref=pair_in.at[l, z],
            send_sem=y_send.at[l, z],
            recv_sem=y_recv.at[l, z],
            device_id={"hist": beside},
            device_id_type=MESH,
        )

    def m_copy(l, z, owner):
        return pltpu.make_async_remote_copy(
            src_ref=merged.at[l, z],
            dst_ref=parts_in.at[l, owner],
            send_sem=p_send.at[l, z],
            recv_sem=p_recv.at[l, owner],
            device_id={"hist": z * inner + side},
            device_id_type=MESH,
        )

    def merge(l, z):
        y_copy(l, z).wait_recv()
        both = part[l, row_of(z * inner + side), :].astype(jnp.float32)
        both = both + pair_in[l, z].astype(jnp.float32)
        merged[l, z] = both.astype(jnp.bfloat16)
        m_copy(l, z, line).start()

    def build_keys():
        lane = lax.broadcasted_iota(jnp.int32, (LANES, LANES), 1)
        lane8 = lax.broadcasted_iota(jnp.int32, (blocks, LANES), 1)
        row8 = lax.broadcasted_iota(jnp.int32, (blocks, LANES), 0)
        base_of = (DH, 0)
        seen = []
        gone = []
        for base in base_of:
            held = jnp.zeros((blocks, LANES), jnp.float32)
            for m in range(micro):
                column = jnp.zeros((blocks, LANES), jnp.float32)
                for b in range(blocks):
                    value = (vis[m, b] - 1).astype(jnp.float32) * BIG
                    column = jnp.where(row8 == b, value, column)
                held = jnp.where(lane8 == base + 2 + m, column, held)
            seen.append(held)
            is_micro = (lane8 >= base + 2) & (lane8 < base + 2 + micro)
            gone.append(jnp.where(is_micro & (row8 == 0), -BIG, 0.0))
        for l in range(layers):
            for h in range(heads):
                base = base_of[h % PER]
                half = rab[l][:, h : h + 1] * 0.5
                high = half.astype(jnp.bfloat16).astype(jnp.float32)
                low = half - high
                lane_nb = lane[:nb]
                bias = jnp.where(lane_nb == base, high, jnp.where(lane_nb == base + 1, low, 0.0))
                fill = jnp.zeros((LANES - nb - 2 * blocks, LANES), jnp.float32)
                whole = jnp.concatenate([bias, seen[h % PER], gone[h % PER], fill], axis=0)
                start = (l * heads + h) * LANES
                table[:, start : start + LANES] = whole.astype(jnp.bfloat16)

        row = lax.broadcasted_iota(jnp.int32, (LANES, key_chunk), 0)
        spot = lax.broadcasted_iota(jnp.int32, (LANES, key_chunk), 1)
        lane_k = lax.broadcasted_iota(jnp.int32, (key_chunk, LANES), 1)
        length = hlen[0]
        for c in range(hist_dev // key_chunk):
            span = slice(c * key_chunk, (c + 1) * key_chunk)
            place = spot + c * key_chunk
            here = (
                (row == bucket[:, span])
                | (row == nb + place // BLOCK)
                | ((row == nb + blocks) & (place >= length))
            )
            events[span, :] = jnp.where(here, 1.0, 0.0).T.astype(jnp.bfloat16)
        load_k.wait()

        def chunk(c, carry):
            span = pl.ds(pl.multiple_of(c * key_chunk, key_chunk), key_chunk)
            spread = events[span, :]
            for l in range(layers):
                for h in range(heads):
                    start = (l * heads + h) * LANES
                    extra = dot(spread, table[:, start : start + LANES])
                    p = h // PER
                    tile = keys[l, span, p * LANES : (p + 1) * LANES].astype(jnp.float32)
                    mine = (lane_k < DH) if h % PER == 0 else (lane_k >= DH)
                    kaug[l, h, span, :] = jnp.where(mine, tile, extra).astype(jnp.bfloat16)
            return carry

        lax.fori_loop(0, hist_dev // key_chunk, chunk, 0)

    lane_q = lax.broadcasted_iota(jnp.int32, (group_rows, LANES), 1)
    row_q = lax.broadcasted_iota(jnp.int32, (group_rows, LANES), 0)
    lane_a = lax.broadcasted_iota(jnp.int32, (group_rows, LANES), 1)

    def attend(l, g):
        span = pl.ds(pl.multiple_of(g * group_rows, group_rows), group_rows)
        which = (row_q + g * group_rows) // micro_rows
        for h in range(heads):
            p = h // PER
            base = DH if h % PER == 0 else 0
            tile = qall[l, span, p * LANES : (p + 1) * LANES].astype(jnp.float32)
            ones = (lane_q == base) | (lane_q == base + 1) | (lane_q == base + 2 + which)
            mine = (lane_q < DH) if h % PER == 0 else (lane_q >= DH)
            qaug[h] = jnp.where(mine, tile, jnp.where(ones, 1.0, 0.0)).astype(jnp.bfloat16)
        acc[...] = jnp.zeros_like(acc)

        def chunk(c, carry):
            keys_at = pl.ds(pl.multiple_of(c * key_chunk, key_chunk), key_chunk)
            for p in range(pairs):
                value = vals[l, keys_at, p * LANES : (p + 1) * LANES]
                found = []
                for e in range(PER):
                    h = p * PER + e
                    y = lax.dot_general(
                        qaug[h],
                        kaug[l, h, keys_at, :],
                        (((1,), (1,)), ((), ())),
                        preferred_element_type=jnp.float32,
                    ).astype(jnp.bfloat16)
                    weight = y * (jnp.tanh(y) + 1.0)
                    found.append(dot(weight, value))
                acc[:, p * LANES : (p + 1) * LANES] += jnp.where(lane_a < DH, found[0], found[1])
            return carry

        lax.fori_loop(0, hist_dev // key_chunk, chunk, 0)
        part[l, span, :] = acc[...].astype(jnp.bfloat16)

    block_row = lax.broadcasted_iota(jnp.int32, (wl, wl), 0) // DH
    block_col = lax.broadcasted_iota(jnp.int32, (wl, wl), 1) // DH
    same_head = jnp.where(block_row == block_col, 1.0, 0.0).astype(jnp.bfloat16)

    stream = cand[...].astype(jnp.float32)
    for l in range(layers):
        average = jnp.mean(stream, axis=-1, keepdims=True)
        centred = stream - average
        variance = jnp.mean(centred * centred, axis=-1, keepdims=True)
        normed = (centred * lax.rsqrt(variance + epsilon)).astype(jnp.bfloat16)

        def project(i):
            return silu(dot(normed, w_in[l, :, i * wl : (i + 1) * wl])).astype(jnp.bfloat16)

        queries = project(0).astype(jnp.float32)
        qall[l, row_of(me), :] = (queries * (0.5 * DH**-0.5)).astype(jnp.bfloat16)
        if l == 0:
            pl.semaphore_wait(barrier, n)
        if relay:
            for j in range(1, outer):
                z = lax.rem(line + outer - j, outer)
                q_copy(l, z * inner + side, me).start()
                q_copy(l, z * inner + (inner - 1 - side), me).start()
            q_copy(l, beside, me).start()
        else:
            for j in range(1, n):
                q_copy(l, lax.rem(me + j, n), me).start()
        keys_new = project(1).astype(jnp.float32)
        values_new = project(2).astype(jnp.float32)
        gates = project(3)
        gate_send[l] = gates
        gate_copy = to_head(gate_send.at[l], gate_in.at[l], 2 * l)
        gate_copy.start()
        if l == 0:
            w_copy = to_head(w_out, w_other, 2 * layers)
            w_copy.start()
        product = queries * keys_new
        high = product.astype(jnp.bfloat16)
        low = (product - high.astype(jnp.float32)).astype(jnp.bfloat16)
        own_score = dot(high, same_head) + dot(low, same_head)
        own = silu(own_score * (DH**-0.5)) * values_new
        if l == 0:
            build_keys()
            load_v.wait()

        def group(t, carry):
            g = lax.rem(me // per_group + t, groups)
            for i in range(per_group):
                s = g * per_group + i

                @pl.when(s != me)
                def _():
                    q_copy(l, s, s).wait_recv()

            attend(l, g)
            for i in range(per_group):
                s = g * per_group + i

                @pl.when(s != me)
                def _():
                    p_copy(l, s, me).start()

            return carry

        def relayed(t, carry):
            z = lax.rem(line + t + 1, outer)
            for i in range(inner):
                s = z * inner + i

                @pl.when(s != me)
                def _():
                    q_copy(l, s, s).wait_recv()

            attend(l, z)
            y_copy(l, z).start()

            @pl.when(t > 0)
            def _():
                merge(l, lax.rem(line + t, outer))

            return carry

        if relay:
            lax.fori_loop(0, outer, relayed, 0)
            y_copy(l, line).wait_recv()
            history = part[l, row_of(me), :].astype(jnp.float32)
            history = history + pair_in[l, line].astype(jnp.float32)
            for j in range(1, outer):
                z = lax.rem(line + outer - j, outer)
                m_copy(l, z, z).wait_recv()
                history = history + parts_in[l, z].astype(jnp.float32)
        else:
            lax.fori_loop(0, groups, group, 0)
            history = part[l, row_of(me), :].astype(jnp.float32)
            for j in range(1, n):
                s = lax.rem(me + j, n)
                p_copy(l, s, s).wait_recv()
                history = history + parts_in[l, s].astype(jnp.float32)
        attended = history + own
        att_send[l] = attended
        att_copy = to_head(att_send.at[l], att_in.at[l], 2 * l + 1)
        att_copy.start()
        if l == 0:
            w_copy.wait_recv()
        gate_copy.wait_recv()
        att_copy.wait_recv()
        theirs = att_in[l]
        width = 2 * wl
        mean = (
            jnp.sum(attended, axis=-1, keepdims=True) + jnp.sum(theirs, axis=-1, keepdims=True)
        ) / width
        square = (
            jnp.sum(attended * attended, axis=-1, keepdims=True)
            + jnp.sum(theirs * theirs, axis=-1, keepdims=True)
        ) / width
        rstd = lax.rsqrt(square - mean * mean + epsilon)
        gated = ((attended - mean) * rstd * gates.astype(jnp.float32)).astype(jnp.bfloat16)
        gated_other = ((theirs - mean) * rstd * gate_in[l].astype(jnp.float32)).astype(
            jnp.bfloat16
        )
        stream = stream + (dot(gated, w_out[l]) + dot(gated_other, w_other[l]))
        gate_copy.wait_send()
        att_copy.wait_send()
        if l == 0:
            w_copy.wait_send()
        if relay:
            for j in range(1, n):
                q_copy(l, lax.rem(me + j, n), me).wait_send()
            y_copy(l, line).wait_send()
            for j in range(1, outer):
                z = lax.rem(line + j, outer)
                y_copy(l, z).wait_send()
                m_copy(l, z, line).wait_send()
        else:
            for j in range(1, n):
                s = lax.rem(me + j, n)
                q_copy(l, s, me).wait_send()
                p_copy(l, s, me).wait_send()
    out[...] = stream.astype(out.dtype)


def shards(
    n, inner, candidates, key_cache, value_cache, w_in, w_out, rab_table, hist_len, hist_bucket, visible
):
    layers, hist_dev, wl = key_cache.shape
    rows, d = candidates.shape
    heads = wl // DH
    total = n * rows
    group_rows = min(GROUP_ROWS, total)
    bf16, f32 = jnp.bfloat16, jnp.float32
    vmem = pl.BlockSpec(memory_space=pltpu.VMEM)
    smem = pl.BlockSpec(memory_space=pltpu.SMEM)
    hbm = pl.BlockSpec(memory_space=pl.ANY)
    dma = pltpu.SemaphoreType.DMA
    return pl.pallas_call(
        functools.partial(kernel, n, inner),
        out_shape=jax.ShapeDtypeStruct((rows, d), bf16),
        in_specs=[vmem, vmem, hbm, hbm, vmem, vmem, vmem, smem, smem],
        out_specs=vmem,
        scratch_shapes=[
            pltpu.VMEM((layers, hist_dev, wl), bf16),
            pltpu.VMEM((layers, hist_dev, wl), bf16),
            pltpu.VMEM((layers, heads, hist_dev, LANES), bf16),
            pltpu.VMEM((LANES, layers * heads * LANES), bf16),
            pltpu.VMEM((hist_dev, LANES), bf16),
            pltpu.VMEM(w_out.shape, bf16),
            pltpu.VMEM((layers, total, wl), bf16),
            pltpu.VMEM((heads, group_rows, LANES), bf16),
            pltpu.VMEM((layers, total, wl), bf16),
            pltpu.VMEM((layers, n, rows, wl), bf16),
            pltpu.VMEM((layers, n // inner, rows, wl), bf16),
            pltpu.VMEM((layers, n // inner, rows, wl), bf16),
            pltpu.VMEM((group_rows, wl), f32),
            pltpu.VMEM((layers, rows, wl), f32),
            pltpu.VMEM((layers, rows, wl), f32),
            pltpu.VMEM((layers, rows, wl), bf16),
            pltpu.VMEM((layers, rows, wl), bf16),
            dma((2,)),
            dma((layers, n)),
            dma((layers, n)),
            dma((layers, n)),
            dma((layers, n)),
            dma((layers, n)),
            dma((layers, n)),
            dma((2 * layers + 1,)),
            dma((2 * layers + 1,)),
        ],
        compiler_params=pltpu.CompilerParams(
            collective_id=0, has_side_effects=True, vmem_limit_bytes=48 * 1024 * 1024
        ),
    )(
        candidates,
        w_in.reshape(layers, d, 4 * wl),
        key_cache,
        value_cache,
        w_out,
        rab_table,
        hist_bucket.reshape(1, hist_dev),
        hist_len,
        visible,
    )


def inner_of(mesh):
    n = mesh.shape["hist"]
    if n % 2 or n < 4:
        return 1
    index = [slice(None) if name == "hist" else 0 for name in mesh.axis_names]
    spots = [getattr(device, "coords", None) for device in mesh.devices[tuple(index)][:3]]
    if any(spot is None for spot in spots):
        return 1
    apart = [sum(abs(a - b) for a, b in zip(spots[0], spot)) for spot in spots[1:]]
    return 2 if apart == [1, 1] else 1


def solution(mesh):
    placed = (
        P(("users", "hist"), None),
        P(None, ("users", "hist"), "head"),
        P(None, ("users", "hist"), "head"),
        P(None, None, None, "head"),
        P(None, "head", None),
        P(None, None, "head"),
        P(("users", "hist")),
        P(("users", "hist")),
        P(None, ("users", "hist")),
    )
    return jax.shard_map(
        functools.partial(shards, mesh.shape["hist"], inner_of(mesh)),
        mesh=mesh,
        in_specs=placed,
        out_specs=P(("users", "hist"), None),
        check_vma=False,
    )
```

```python
import functools

import jax
import jax.numpy as jnp
from jax import lax
from jax.experimental import pallas as pl
from jax.experimental.pallas import tpu as pltpu
from jax.sharding import PartitionSpec as P

DH = 64
BLOCK = 256
LANES = 128
PER = LANES // DH
GROUP_ROWS = 256
KEY_CHUNK = 2048
BIG = 16384.0
MESH = pl.DeviceIdType.MESH

epsilon = 1e-05


def silu(v):
    return v / (1.0 + jnp.exp(-v))


def dot(a, b):
    return jnp.dot(a, b, preferred_element_type=jnp.float32)


def kernel(
    n,
    inner,
    cand,
    w_in,
    key_hbm,
    val_hbm,
    w_out,
    rab,
    bucket,
    hlen,
    vis,
    out,
    keys,
    vals,
    kaug,
    table,
    events,
    w_other,
    qall,
    qaug,
    part,
    parts_in,
    pair_in,
    merged,
    acc,
    att_send,
    att_in,
    gate_send,
    gate_in,
    load_sem,
    q_send,
    q_recv,
    p_send,
    p_recv,
    y_send,
    y_recv,
    h_send,
    h_recv,
):
    me = lax.axis_index("hist")
    other = 1 - lax.axis_index("head")
    layers, hist_dev, wl = key_hbm.shape
    rows, d = cand.shape
    heads = wl // DH
    pairs = wl // LANES
    nb = rab.shape[1]
    micro, blocks = vis.shape
    total = n * rows
    micro_rows = total // micro
    group_rows = min(GROUP_ROWS, total)
    per_group = group_rows // rows
    groups = n // per_group
    outer = n // inner
    relay = inner == 2 and per_group == inner
    line, side = me // inner, lax.rem(me, inner)
    beside = line * inner + (inner - 1 - side)
    key_chunk = min(KEY_CHUNK, hist_dev)

    load_k = pltpu.make_async_copy(key_hbm, keys, load_sem.at[0])
    load_v = pltpu.make_async_copy(val_hbm, vals, load_sem.at[1])
    load_k.start()
    load_v.start()

    barrier = pltpu.get_barrier_semaphore()
    for j in range(1, n):
        pl.semaphore_signal(
            barrier, inc=1, device_id={"hist": lax.rem(me + j, n)}, device_id_type=MESH
        )
    pl.semaphore_signal(barrier, inc=1, device_id={"head": other}, device_id_type=MESH)

    def to_head(src, dst, index):
        return pltpu.make_async_remote_copy(
            src_ref=src,
            dst_ref=dst,
            send_sem=h_send.at[index],
            recv_sem=h_recv.at[index],
            device_id={"head": other},
            device_id_type=MESH,
        )

    def row_of(s):
        return pl.ds(pl.multiple_of(s * rows, rows), rows)

    def q_copy(l, s, owner):
        return pltpu.make_async_remote_copy(
            src_ref=qall.at[l, row_of(owner)],
            dst_ref=qall.at[l, row_of(owner)],
            send_sem=q_send.at[l, s],
            recv_sem=q_recv.at[l, owner],
            device_id={"hist": s},
            device_id_type=MESH,
        )

    def p_copy(l, s, owner):
        return pltpu.make_async_remote_copy(
            src_ref=part.at[l, row_of(s)],
            dst_ref=parts_in.at[l, owner],
            send_sem=p_send.at[l, s],
            recv_sem=p_recv.at[l, owner],
            device_id={"hist": s},
            device_id_type=MESH,
        )

    def y_copy(l, z):
        return pltpu.make_async_remote_copy(
            src_ref=part.at[l, row_of(z * inner + (inner - 1 - side))],
            dst_ref=pair_in.at[l, z],
            send_sem=y_send.at[l, z],
            recv_sem=y_recv.at[l, z],
            device_id={"hist": beside},
            device_id_type=MESH,
        )

    def m_copy(l, z, owner):
        return pltpu.make_async_remote_copy(
            src_ref=merged.at[l, z],
            dst_ref=parts_in.at[l, owner],
            send_sem=p_send.at[l, z],
            recv_sem=p_recv.at[l, owner],
            device_id={"hist": z * inner + side},
            device_id_type=MESH,
        )

    def merge(l, z):
        y_copy(l, z).wait_recv()
        both = part[l, row_of(z * inner + side), :].astype(jnp.float32)
        both = both + pair_in[l, z].astype(jnp.float32)
        merged[l, z] = both.astype(jnp.bfloat16)
        m_copy(l, z, line).start()

    def build_keys():
        lane = lax.broadcasted_iota(jnp.int32, (LANES, LANES), 1)
        lane8 = lax.broadcasted_iota(jnp.int32, (blocks, LANES), 1)
        row8 = lax.broadcasted_iota(jnp.int32, (blocks, LANES), 0)
        base_of = (DH, 0)
        seen = []
        gone = []
        for base in base_of:
            held = jnp.zeros((blocks, LANES), jnp.float32)
            for m in range(micro):
                column = jnp.zeros((blocks, LANES), jnp.float32)
                for b in range(blocks):
                    value = (vis[m, b] - 1).astype(jnp.float32) * BIG
                    column = jnp.where(row8 == b, value, column)
                held = jnp.where(lane8 == base + 2 + m, column, held)
            seen.append(held)
            is_micro = (lane8 >= base + 2) & (lane8 < base + 2 + micro)
            gone.append(jnp.where(is_micro & (row8 == 0), -BIG, 0.0))
        for l in range(layers):
            for h in range(heads):
                base = base_of[h % PER]
                half = rab[l][:, h : h + 1] * 0.5
                high = half.astype(jnp.bfloat16).astype(jnp.float32)
                low = half - high
                lane_nb = lane[:nb]
                bias = jnp.where(lane_nb == base, high, jnp.where(lane_nb == base + 1, low, 0.0))
                fill = jnp.zeros((LANES - nb - 2 * blocks, LANES), jnp.float32)
                whole = jnp.concatenate([bias, seen[h % PER], gone[h % PER], fill], axis=0)
                start = (l * heads + h) * LANES
                table[:, start : start + LANES] = whole.astype(jnp.bfloat16)

        row = lax.broadcasted_iota(jnp.int32, (LANES, key_chunk), 0)
        spot = lax.broadcasted_iota(jnp.int32, (LANES, key_chunk), 1)
        lane_k = lax.broadcasted_iota(jnp.int32, (key_chunk, LANES), 1)
        length = hlen[0]
        for c in range(hist_dev // key_chunk):
            span = slice(c * key_chunk, (c + 1) * key_chunk)
            place = spot + c * key_chunk
            here = (
                (row == bucket[:, span])
                | (row == nb + place // BLOCK)
                | ((row == nb + blocks) & (place >= length))
            )
            events[span, :] = jnp.where(here, 1.0, 0.0).T.astype(jnp.bfloat16)
        load_k.wait()

        def chunk(c, carry):
            span = pl.ds(pl.multiple_of(c * key_chunk, key_chunk), key_chunk)
            spread = events[span, :]
            for l in range(layers):
                for h in range(heads):
                    start = (l * heads + h) * LANES
                    extra = dot(spread, table[:, start : start + LANES])
                    p = h // PER
                    tile = keys[l, span, p * LANES : (p + 1) * LANES].astype(jnp.float32)
                    mine = (lane_k < DH) if h % PER == 0 else (lane_k >= DH)
                    kaug[l, h, span, :] = jnp.where(mine, tile, extra).astype(jnp.bfloat16)
            return carry

        lax.fori_loop(0, hist_dev // key_chunk, chunk, 0)

    lane_q = lax.broadcasted_iota(jnp.int32, (group_rows, LANES), 1)
    row_q = lax.broadcasted_iota(jnp.int32, (group_rows, LANES), 0)
    lane_a = lax.broadcasted_iota(jnp.int32, (group_rows, LANES), 1)

    def attend(l, g):
        span = pl.ds(pl.multiple_of(g * group_rows, group_rows), group_rows)
        which = (row_q + g * group_rows) // micro_rows
        for h in range(heads):
            p = h // PER
            base = DH if h % PER == 0 else 0
            tile = qall[l, span, p * LANES : (p + 1) * LANES].astype(jnp.float32)
            ones = (lane_q == base) | (lane_q == base + 1) | (lane_q == base + 2 + which)
            mine = (lane_q < DH) if h % PER == 0 else (lane_q >= DH)
            qaug[h] = jnp.where(mine, tile, jnp.where(ones, 1.0, 0.0)).astype(jnp.bfloat16)
        acc[...] = jnp.zeros_like(acc)

        def chunk(c, carry):
            keys_at = pl.ds(pl.multiple_of(c * key_chunk, key_chunk), key_chunk)
            for p in range(pairs):
                value = vals[l, keys_at, p * LANES : (p + 1) * LANES]
                found = []
                for e in range(PER):
                    h = p * PER + e
                    y = lax.dot_general(
                        qaug[h],
                        kaug[l, h, keys_at, :],
                        (((1,), (1,)), ((), ())),
                        preferred_element_type=jnp.float32,
                    ).astype(jnp.bfloat16)
                    weight = y * (jnp.tanh(y) + 1.0)
                    found.append(dot(weight, value))
                acc[:, p * LANES : (p + 1) * LANES] += jnp.where(lane_a < DH, found[0], found[1])
            return carry

        lax.fori_loop(0, hist_dev // key_chunk, chunk, 0)
        part[l, span, :] = acc[...].astype(jnp.bfloat16)

    block_row = lax.broadcasted_iota(jnp.int32, (wl, wl), 0) // DH
    block_col = lax.broadcasted_iota(jnp.int32, (wl, wl), 1) // DH
    same_head = jnp.where(block_row == block_col, 1.0, 0.0).astype(jnp.bfloat16)

    stream = cand[...].astype(jnp.float32)
    for l in range(layers):
        average = jnp.mean(stream, axis=-1, keepdims=True)
        centred = stream - average
        variance = jnp.mean(centred * centred, axis=-1, keepdims=True)
        normed = (centred * lax.rsqrt(variance + epsilon)).astype(jnp.bfloat16)

        def project(i):
            return silu(dot(normed, w_in[l, :, i * wl : (i + 1) * wl])).astype(jnp.bfloat16)

        queries = project(0).astype(jnp.float32)
        qall[l, row_of(me), :] = (queries * (0.5 * DH**-0.5)).astype(jnp.bfloat16)
        if l == 0:
            pl.semaphore_wait(barrier, n)
        if relay:
            for j in range(1, outer):
                z = lax.rem(line + outer - j, outer)
                q_copy(l, z * inner + side, me).start()
                q_copy(l, z * inner + (inner - 1 - side), me).start()
            q_copy(l, beside, me).start()
        else:
            for j in range(1, n):
                q_copy(l, lax.rem(me + j, n), me).start()
        keys_new = project(1).astype(jnp.float32)
        values_new = project(2).astype(jnp.float32)
        gates = project(3)
        gate_send[l] = gates
        gate_copy = to_head(gate_send.at[l], gate_in.at[l], 2 * l)
        gate_copy.start()
        if l == 0:
            w_copy = to_head(w_out, w_other, 2 * layers)
            w_copy.start()
        product = queries * keys_new
        high = product.astype(jnp.bfloat16)
        low = (product - high.astype(jnp.float32)).astype(jnp.bfloat16)
        own_score = dot(high, same_head) + dot(low, same_head)
        own = silu(own_score * (DH**-0.5)) * values_new
        if l == 0:
            build_keys()
            load_v.wait()

        def group(t, carry):
            g = lax.rem(me // per_group + t, groups)
            for i in range(per_group):
                s = g * per_group + i

                @pl.when(s != me)
                def _():
                    q_copy(l, s, s).wait_recv()

            attend(l, g)
            for i in range(per_group):
                s = g * per_group + i

                @pl.when(s != me)
                def _():
                    p_copy(l, s, me).start()

            return carry

        def relayed(t, carry):
            z = lax.rem(line + t + 1, outer)
            for i in range(inner):
                s = z * inner + i

                @pl.when(s != me)
                def _():
                    q_copy(l, s, s).wait_recv()

            attend(l, z)
            y_copy(l, z).start()

            @pl.when(t > 0)
            def _():
                merge(l, lax.rem(line + t, outer))

            return carry

        if relay:
            lax.fori_loop(0, outer, relayed, 0)
            y_copy(l, line).wait_recv()
            history = part[l, row_of(me), :].astype(jnp.float32)
            history = history + pair_in[l, line].astype(jnp.float32)
            for j in range(1, outer):
                z = lax.rem(line + outer - j, outer)
                m_copy(l, z, z).wait_recv()
                history = history + parts_in[l, z].astype(jnp.float32)
        else:
            lax.fori_loop(0, groups, group, 0)
            history = part[l, row_of(me), :].astype(jnp.float32)
            for j in range(1, n):
                s = lax.rem(me + j, n)
                p_copy(l, s, s).wait_recv()
                history = history + parts_in[l, s].astype(jnp.float32)
        attended = history + own
        att_send[l] = attended
        att_copy = to_head(att_send.at[l], att_in.at[l], 2 * l + 1)
        att_copy.start()
        if l == 0:
            w_copy.wait_recv()
        gate_copy.wait_recv()
        att_copy.wait_recv()
        theirs = att_in[l]
        width = 2 * wl
        mean = (
            jnp.sum(attended, axis=-1, keepdims=True) + jnp.sum(theirs, axis=-1, keepdims=True)
        ) / width
        square = (
            jnp.sum(attended * attended, axis=-1, keepdims=True)
            + jnp.sum(theirs * theirs, axis=-1, keepdims=True)
        ) / width
        rstd = lax.rsqrt(square - mean * mean + epsilon)
        gated = ((attended - mean) * rstd * gates.astype(jnp.float32)).astype(jnp.bfloat16)
        gated_other = ((theirs - mean) * rstd * gate_in[l].astype(jnp.float32)).astype(
            jnp.bfloat16
        )
        stream = stream + (dot(gated, w_out[l]) + dot(gated_other, w_other[l]))
        gate_copy.wait_send()
        att_copy.wait_send()
        if l == 0:
            w_copy.wait_send()
        if relay:
            for j in range(1, n):
                q_copy(l, lax.rem(me + j, n), me).wait_send()
            y_copy(l, line).wait_send()
            for j in range(1, outer):
                z = lax.rem(line + j, outer)
                y_copy(l, z).wait_send()
                m_copy(l, z, line).wait_send()
        else:
            for j in range(1, n):
                s = lax.rem(me + j, n)
                q_copy(l, s, me).wait_send()
                p_copy(l, s, me).wait_send()
    out[...] = stream.astype(out.dtype)


def shards(
    n, inner, candidates, key_cache, value_cache, w_in, w_out, rab_table, hist_len, hist_bucket, visible
):
    layers, hist_dev, wl = key_cache.shape
    rows, d = candidates.shape
    heads = wl // DH
    total = n * rows
    group_rows = min(GROUP_ROWS, total)
    bf16, f32 = jnp.bfloat16, jnp.float32
    vmem = pl.BlockSpec(memory_space=pltpu.VMEM)
    smem = pl.BlockSpec(memory_space=pltpu.SMEM)
    hbm = pl.BlockSpec(memory_space=pltpu.HBM)
    dma = pltpu.SemaphoreType.DMA
    return pl.pallas_call(
        functools.partial(kernel, n, inner),
        out_shape=jax.ShapeDtypeStruct((rows, d), bf16),
        in_specs=[vmem, vmem, hbm, hbm, vmem, vmem, vmem, smem, smem],
        out_specs=vmem,
        scratch_shapes=[
            pltpu.VMEM((layers, hist_dev, wl), bf16),
            pltpu.VMEM((layers, hist_dev, wl), bf16),
            pltpu.VMEM((layers, heads, hist_dev, LANES), bf16),
            pltpu.VMEM((LANES, layers * heads * LANES), bf16),
            pltpu.VMEM((hist_dev, LANES), bf16),
            pltpu.VMEM(w_out.shape, bf16),
            pltpu.VMEM((layers, total, wl), bf16),
            pltpu.VMEM((heads, group_rows, LANES), bf16),
            pltpu.VMEM((layers, total, wl), bf16),
            pltpu.VMEM((layers, n, rows, wl), bf16),
            pltpu.VMEM((layers, n // inner, rows, wl), bf16),
            pltpu.VMEM((layers, n // inner, rows, wl), bf16),
            pltpu.VMEM((group_rows, wl), f32),
            pltpu.VMEM((layers, rows, wl), f32),
            pltpu.VMEM((layers, rows, wl), f32),
            pltpu.VMEM((layers, rows, wl), bf16),
            pltpu.VMEM((layers, rows, wl), bf16),
            dma((2,)),
            dma((layers, n)),
            dma((layers, n)),
            dma((layers, n)),
            dma((layers, n)),
            dma((layers, n)),
            dma((layers, n)),
            dma((2 * layers + 1,)),
            dma((2 * layers + 1,)),
        ],
        compiler_params=pltpu.CompilerParams(
            collective_id=0, has_side_effects=True, vmem_limit_bytes=48 * 1024 * 1024
        ),
    )(
        candidates,
        w_in.reshape(layers, d, 4 * wl),
        key_cache,
        value_cache,
        w_out,
        rab_table,
        hist_bucket.reshape(1, hist_dev),
        hist_len,
        visible,
    )


def inner_of(mesh):
    n = mesh.shape["hist"]
    if n % 2 or n < 4:
        return 1
    index = [slice(None) if name == "hist" else 0 for name in mesh.axis_names]
    spots = [getattr(device, "coords", None) for device in mesh.devices[tuple(index)][:3]]
    if any(spot is None for spot in spots):
        return 1
    apart = [sum(abs(a - b) for a, b in zip(spots[0], spot)) for spot in spots[1:]]
    return 2 if apart == [1, 1] else 1


def solution(mesh):
    placed = (
        P(("users", "hist"), None),
        P(None, ("users", "hist"), "head"),
        P(None, ("users", "hist"), "head"),
        P(None, None, None, "head"),
        P(None, "head", None),
        P(None, None, "head"),
        P(("users", "hist")),
        P(("users", "hist")),
        P(None, ("users", "hist")),
    )
    return jax.shard_map(
        functools.partial(shards, mesh.shape["hist"], inner_of(mesh)),
        mesh=mesh,
        in_specs=placed,
        out_specs=P(("users", "hist"), None),
        check_vma=False,
    )
```
